32 devices in a mesh: row: 8 (over z, y), col: 4 (over x, core).
Axes of the slice: x: 2, y: 2, z: 4, core: 2. Of those that a mesh axis runs over, the one named last changes fastest.
Arguments:
- points: float32 [8, 32768], P(None, ('row', 'col')), may hold values from -4 to 4
- lengthscale: float32 [8], replicated, may hold values from 0.7 to 1.4
- noise: float32 [1], replicated, may hold values from 0.1 to 1
- iterate: float32 [16, 32768], P(None, ('row', 'col')), may hold values from -6 to 6
- residual: float32 [16, 32768], P(None, ('row', 'col')), may hold values from -8 to 8
- direction: float32 [16, 32768], P(None, ('row', 'col')), may hold values from -8 to 8
- previous_rz: float32 [16], replicated, may hold values from 32768 to 131072
- members: int32 [32, 2048], replicated, may hold values from 0 to 32768, as said below
- slot_cluster: int32 [32], P('row'), may hold values from 0 to 31, as said below
- factors: bfloat16 [32, 2048, 2048], P('row', None, 'col'), may hold values from -1 to 3, as said below
Outputs:
- new_iterate: float32 [16, 32768], P(None, ('row', 'col'))
- new_residual: float32 [16, 32768], P(None, ('row', 'col'))
- new_direction: float32 [16, 32768], P(None, ('row', 'col'))
- rz_new: float32 [16], replicated
The draws below stay inside these ranges and needn't reach their ends.
Inputs may be any that keep to these rules, and one draw needn't show every extreme that they name: `members`: the first 1024 entries of row c are the points c * 1024 to c * 1024 + 1023 in increasing order, the points cluster c owns. They are followed by margin points of one other cluster, distinct from each other, and then by padding entries equal to 32768. Some row has no padding. `slot_cluster`: A permutation of the clusters in which some slot s holds cluster s. `factors`: each slot's matrix is lower triangular with a diagonal of 1 or more.
All inputs are finite; a program needn't handle non-finite values.
Results may differ from the reference program's by a relative error of at most 0.0047.
Values may be sent and summed in bfloat16 or wider, within the bound.
A program may use at most 192 MiB of HBM per device.

```python
import math
import jax
import jax.numpy as jnp
from jax import lax

DIM = 8
PROBES = 16
CORE = 1024
CL = 2048
POINTS = 32768
NCLUST = 32


def ramp_field(seed_key):
    shape = (PROBES, POINTS)
    ramp = 0.5 + jnp.arange(POINTS, dtype=jnp.float32) / POINTS
    values = jax.random.truncated_normal(seed_key, -5.0, 5.0, shape, jnp.float32)
    return ramp[None, :] * values


def draw_direction(key, part):
    return ramp_field(jax.random.fold_in(key, 101)).astype(jnp.float32)


def draw_residual(key, part):
    return ramp_field(jax.random.fold_in(key, 202)).astype(jnp.float32)


def draw_slot_cluster(key, part):
    shuffled = jax.random.permutation(jax.random.fold_in(key, 909), NCLUST).astype(jnp.int32)
    home_slot = jax.random.randint(jax.random.fold_in(key, 910), (), 0, NCLUST).astype(jnp.int32)
    slot_index = jnp.arange(NCLUST, dtype=jnp.int32)
    found_at = jnp.sum(jnp.where(shuffled == home_slot, slot_index, 0)).astype(jnp.int32)
    displaced = jnp.sum(jnp.where(slot_index == home_slot, shuffled, 0)).astype(jnp.int32)
    swapped = jnp.where(slot_index == home_slot, home_slot, jnp.where(slot_index == found_at, displaced, shuffled))
    return swapped.astype(jnp.int32)


def draw_members(key, part):
    extra = jax.random.randint(jax.random.fold_in(key, 404), (NCLUST,), (CL - CORE) // 4, CL - CORE + 1).astype(jnp.int32)
    extra = extra.at[0].set(CL - CORE)
    hop = jax.random.randint(jax.random.fold_in(key, 707), (NCLUST, 1), 1, NCLUST).astype(jnp.int32)
    begin = jax.random.randint(jax.random.fold_in(key, 808), (NCLUST, 1), 0, CORE).astype(jnp.int32)
    cluster = jnp.arange(NCLUST, dtype=jnp.int32)[:, None]
    position = jnp.arange(CL, dtype=jnp.int32)[None, :]
    core_pick = cluster * CORE + jnp.minimum(position, CORE - 1)
    other = (cluster + hop) % NCLUST
    halo_pick = other * CORE + (position - CORE + begin) % CORE
    padding = jnp.full((NCLUST, CL), POINTS, jnp.int32)
    return jnp.where(position < CORE, core_pick, jnp.where(position < CORE + extra[:, None], halo_pick, padding)).astype(jnp.int32)


def draw_factors(key, part):
    shape = (NCLUST, CL, CL)
    row_index = jnp.arange(CL)[:, None]
    column_index = jnp.arange(CL)[None, :]
    lower_key = jax.random.fold_in(key, 505)
    diagonal_key = jax.random.fold_in(key, 606)
    lower = 0.5 * jax.random.truncated_normal(lower_key, -4.0, 4.0, shape, jnp.float32) / jnp.sqrt(jnp.float32(CL))
    diagonal = jax.random.uniform(diagonal_key, shape, jnp.float32, 1.0, 2.0)
    zeros_upper = jnp.zeros(shape, jnp.float32)
    values = jnp.where(row_index > column_index, lower, jnp.where(row_index == column_index, diagonal, zeros_upper))
    return values.astype(jnp.bfloat16)


def steps_of(own_key, dims, cuts, smallest, largest):
    factor_of = 1.0
    for axis_at, blocks in cuts:
        steps = jax.random.uniform(jax.random.fold_in(jax.random.fold_in(own_key, 6), axis_at), (blocks,), jnp.float32, smallest / len(cuts), largest / len(cuts))
        factor_of = factor_of * jnp.repeat(jnp.exp(steps), dims[axis_at] // blocks).reshape((-1,) + (1,) * (len(dims) - 1 - axis_at))
    return factor_of


def scatter_about(key, extent, scale, limit, cuts=(), held_as=jnp.bfloat16):
    drawn = jax.random.normal(key, extent, jnp.float32) * scale
    if len(cuts) > 0:
        drawn = steps_of(key, extent, cuts, -0.22, 0.18) * drawn
    return jnp.clip(drawn, min=-limit, max=limit).astype(held_as)


def setup_inputs(seed: int = 0) -> dict:
    key_list = jax.random.split(jax.random.key(seed), 11)
    points = scatter_about(key_list[0], (DIM, POINTS), 1.0, 4.0, ((1, 32),), jnp.float32)
    lengthscale = jnp.clip(jnp.exp(jax.random.uniform(key_list[1], (DIM,), jnp.float32, math.log(0.7), math.log(1.4))), 0.7, 1.4)
    noise = jnp.clip(jnp.exp(jax.random.uniform(key_list[2], (1,), jnp.float32, math.log(0.1), math.log(1.0))), 0.1, 1.0)
    iterate = scatter_about(key_list[3], (PROBES, POINTS), 1.0, 6.0, ((1, 32),), jnp.float32)
    residual = draw_residual(jax.random.fold_in(key_list[10], 71), 0)
    direction = draw_direction(jax.random.fold_in(key_list[10], 71), 0)
    previous_rz = jnp.clip(jnp.exp(jax.random.uniform(key_list[6], (PROBES,), jnp.float32, math.log(32768.0), math.log(131072.0))), 32768.0, 131072.0)
    members = draw_members(jax.random.fold_in(key_list[10], 71), 0)
    slot_cluster = draw_slot_cluster(jax.random.fold_in(key_list[10], 71), 0)
    factors = draw_factors(jax.random.fold_in(key_list[10], 71), 0)
    return dict(points=points, lengthscale=lengthscale, noise=noise, iterate=iterate, residual=residual, direction=direction, previous_rz=previous_rz, members=members, slot_cluster=slot_cluster, factors=factors)


def kernel_block(left_points, right_points):
    cross_terms = lax.dot_general(left_points, right_points, (((0,), (0,)), ((), ())), precision=lax.Precision.HIGHEST, preferred_element_type=jnp.float32)
    left_norms = lax.optimization_barrier(jnp.sum(left_points * left_points, axis=0))
    right_norms = lax.optimization_barrier(jnp.sum(right_points * right_points, axis=0))
    squared = jnp.maximum(left_norms[:, None] + right_norms[None, :] - 2.0 * cross_terms, 0.0)
    radius = jnp.sqrt(5.0 * squared)
    return ((1.0 + radius + radius * radius / 3.0) * jnp.exp(-radius)).astype(jnp.bfloat16)

def reference(points, lengthscale, noise, iterate, residual, direction, previous_rz, members, slot_cluster, factors):
    scaled = points / lengthscale[:, None]
    direction_low = direction.astype(jnp.bfloat16)
    block_size = math.gcd(512, POINTS)

    def block_product(offset):
        block_points = lax.dynamic_slice_in_dim(scaled, offset, block_size, 1)
        kernel_tile = kernel_block(block_points, scaled)
        return lax.dot_general(direction_low, kernel_tile, (((1,), (1,)), ((), ())), preferred_element_type=jnp.float32)
    offsets = (jnp.arange(POINTS // block_size) * block_size).astype(jnp.int32)
    products = lax.map(block_product, offsets)
    kernel_image = jnp.transpose(products, (1, 0, 2)).reshape(PROBES, POINTS) + noise[0] * direction
    curvature = lax.optimization_barrier(jnp.sum(direction * kernel_image, axis=1))
    step_size = previous_rz / curvature
    new_iterate = iterate + step_size[:, None] * direction
    new_residual = residual - step_size[:, None] * kernel_image
    residual_low = new_residual.astype(jnp.bfloat16)
    padded = jnp.concatenate([residual_low, jnp.zeros((PROBES, 1), jnp.bfloat16)], axis=1)

    def cluster_apply(slot_index):
        member_ids = members[slot_cluster[slot_index]]
        present = member_ids < POINTS
        gathered = jnp.take(padded, member_ids, axis=1)
        factor = factors[slot_index]
        inner_sum = jnp.dot(gathered, factor.T, preferred_element_type=jnp.float32)
        inner_low = jnp.where(present[None, :], inner_sum, 0.0).astype(jnp.bfloat16)
        outer_values = jnp.dot(inner_low, factor, preferred_element_type=jnp.float32)
        return (outer_values[:, :CORE], member_ids[:CORE])
    core_values, core_ids = lax.map(cluster_apply, jnp.arange(NCLUST, dtype=jnp.int32))
    flat_values = jnp.transpose(core_values, (1, 0, 2)).reshape(PROBES, NCLUST * CORE)
    precond = jnp.zeros((PROBES, POINTS), jnp.float32).at[:, core_ids.reshape(-1)].set(flat_values)
    rz_new = lax.optimization_barrier(jnp.sum(residual_low.astype(jnp.float32) * precond, axis=1))
    new_direction = precond + (rz_new / previous_rz)[:, None] * direction
    return (new_iterate, new_residual, new_direction, rz_new)
```

```python
import math

import jax
import jax.numpy as jnp
from jax import lax
from jax.experimental import pallas as pl
from jax.experimental.pallas import tpu as pltpu
from jax.sharding import PartitionSpec as P

CORE = 1024
MESH = pl.DeviceIdType.MESH
FEATURES = 64
LOG2E = math.log2(math.e)
SPREAD = math.sqrt(5.0) * LOG2E
SHIFT = 1.5 * LOG2E
LIFT = 0.75 * LOG2E * LOG2E
EXPONENT = -math.log2(3.0 * LOG2E * LOG2E)


def exchange(arrays, collective_id):
    sizes = {axis: lax.axis_size(axis) for _, axis, _ in arrays}
    count = len(arrays)
    widest = max(sizes.values())

    def kernel(*refs):
        sources, targets = refs[:count], refs[count : 2 * count]
        send_sem, recv_sem = refs[2 * count :]
        barrier = pltpu.get_barrier_semaphore()
        for axis, size in sizes.items():
            me = lax.axis_index(axis)
            for offset in range(1, size):
                pl.semaphore_signal(
                    barrier,
                    inc=1,
                    device_id={axis: lax.rem(me + offset, size)},
                    device_id_type=MESH,
                )
        pl.semaphore_wait(barrier, sum(size - 1 for size in sizes.values()))
        copies = []
        for offset in range(1, widest):
            for k, (_, axis, mode) in enumerate(arrays):
                size = sizes[axis]
                if offset >= size:
                    continue
                me = lax.axis_index(axis)
                peer = lax.rem(me + offset, size)
                copy = pltpu.make_async_remote_copy(
                    src_ref=sources[k] if mode == "gather" else sources[k].at[peer],
                    dst_ref=targets[k].at[me],
                    send_sem=send_sem.at[k, offset],
                    recv_sem=recv_sem.at[k, offset],
                    device_id={axis: peer},
                    device_id_type=MESH,
                )
                copy.start()
                copies.append(copy)
        for k, (_, axis, mode) in enumerate(arrays):
            me = lax.axis_index(axis)
            targets[k][me] = sources[k][...] if mode == "gather" else sources[k][me]
        for copy in copies:
            copy.wait()

    shapes = []
    for array, axis, mode in arrays:
        shape = (sizes[axis],) + array.shape if mode == "gather" else array.shape
        shapes.append(jax.ShapeDtypeStruct(shape, array.dtype))
    return pl.pallas_call(
        kernel,
        out_shape=shapes,
        in_specs=[pl.BlockSpec(memory_space=pltpu.VMEM)] * count,
        out_specs=[pl.BlockSpec(memory_space=pltpu.VMEM)] * count,
        scratch_shapes=[
            pltpu.SemaphoreType.DMA((count, widest)),
            pltpu.SemaphoreType.DMA((count, widest)),
        ],
        compiler_params=pltpu.CompilerParams(collective_id=collective_id, has_side_effects=True),
    )(*[array for array, _, _ in arrays])


def split_three(values):
    high = values.astype(jnp.bfloat16).astype(jnp.float32)
    rest = values - high
    middle = rest.astype(jnp.bfloat16).astype(jnp.float32)
    return high, middle, rest - middle


def feature_rows(points, left):
    high, middle, low = split_three(points)
    norms = split_three(jnp.sum(points * points, axis=0, keepdims=True))
    row = lax.broadcasted_iota(jnp.int32, points.shape, 0)
    first = 0 if left else 3
    tail = jnp.where(row < 6, 1.0, 0.0)
    for k in range(3):
        tail = jnp.where(row == first + k, norms[k], tail)
    if left:
        parts = [-2.0 * part for part in (high, high, middle, middle, high, low)]
    else:
        parts = [high, middle, high, middle, low, high]
    parts += [tail, jnp.zeros_like(tail)]
    return jnp.concatenate(parts, axis=0)


def tile_kernel(tile, left_points, right_points, vectors, out_ref, left, right):
    rows, _, own_count = right_points.shape
    per_block = own_count // tile

    @pl.when(pl.program_id(0) == 0)
    def _():
        def build(index, carry):
            features = feature_rows(right_points[index], False)
            start = pl.multiple_of(index * own_count, own_count)
            right[pl.ds(start, own_count), :] = jnp.transpose(features).astype(jnp.bfloat16)
            return carry

        lax.fori_loop(0, rows, build, 0)

    left[...] = feature_rows(left_points[0], True).astype(jnp.bfloat16)
    out_ref[...] = jnp.zeros_like(out_ref)

    def step(index, carry):
        start = pl.multiple_of(index * tile, tile)
        squared = jnp.dot(
            right[pl.ds(start, tile), :], left[...], preferred_element_type=jnp.float32
        )
        squared = jnp.maximum(squared, 1e-30)
        radius = squared * lax.rsqrt(squared)
        shifted = radius + SHIFT
        kernel = ((shifted * shifted + LIFT) * jnp.exp2(EXPONENT - radius)).astype(jnp.bfloat16)
        inner = pl.multiple_of(lax.rem(index, per_block) * tile, tile)
        out_ref[0] += jnp.dot(
            vectors[index // per_block, :, pl.ds(inner, tile)],
            kernel,
            preferred_element_type=jnp.float32,
        )
        return carry

    lax.fori_loop(0, rows * per_block, step, 0)


def apply_tile(left_points, right_points, vectors):
    cols, dims, own_count = left_points.shape
    rows, probes, _ = vectors.shape
    tile = math.gcd(512, own_count)

    def kernel(*refs):
        tile_kernel(tile, *refs)

    return pl.pallas_call(
        kernel,
        grid=(cols,),
        out_shape=jax.ShapeDtypeStruct((cols, probes, own_count), jnp.float32),
        in_specs=[
            pl.BlockSpec((1, dims, own_count), lambda i: (i, 0, 0)),
            pl.BlockSpec((rows, dims, own_count), lambda i: (0, 0, 0)),
            pl.BlockSpec((rows, probes, own_count), lambda i: (0, 0, 0)),
        ],
        out_specs=pl.BlockSpec((1, probes, own_count), lambda i: (i, 0, 0)),
        scratch_shapes=[
            pltpu.VMEM((FEATURES, own_count), jnp.bfloat16),
            pltpu.VMEM((rows * own_count, FEATURES), jnp.bfloat16),
        ],
    )(left_points, right_points, vectors)


def greet(sizes):
    barrier = pltpu.get_barrier_semaphore()
    for axis, size in sizes.items():
        me = lax.axis_index(axis)
        for offset in range(1, size):
            pl.semaphore_signal(
                barrier,
                inc=1,
                device_id={axis: lax.rem(me + offset, size)},
                device_id_type=MESH,
            )
    pl.semaphore_wait(barrier, sum(size - 1 for size in sizes.values()))


def push(source, target, send_sem, recv_sem, axis, peer):
    copy = pltpu.make_async_remote_copy(
        src_ref=source,
        dst_ref=target,
        send_sem=send_sem,
        recv_sem=recv_sem,
        device_id={axis: peer},
        device_id_type=MESH,
    )
    copy.start()
    return copy


def spread(source, target, send_sem, recv_sem, axis, size):
    me = lax.axis_index(axis)
    return [
        push(source, target.at[me], send_sem.at[o], recv_sem.at[o], axis, lax.rem(me + o, size))
        for o in range(1, size)
    ]


def total_over(mine, held, send_sem, recv_sem, axis, size):
    copies = spread(mine, held, send_sem, recv_sem, axis, size)
    held[lax.axis_index(axis)] = mine[...]
    for copy in copies:
        copy.wait()
    total = held[0]
    for k in range(1, size):
        total = total + held[k]
    return total


def step_kernel(
    rows,
    cols,
    terms,
    direction,
    residual,
    iterate,
    previous,
    noise,
    new_iterate,
    new_residual,
    everyone,
    parts,
    curve,
    curve_cols,
    curve_rows,
    sems,
    row_sems,
    chip_sems,
    core_sems,
):
    row, col = lax.axis_index("row"), lax.axis_index("col")
    greet({"row": rows, "col": cols})
    copies = [
        push(
            terms.at[lax.rem(col + o, cols)],
            parts.at[col],
            sems.at[0, 0, o],
            sems.at[1, 0, o],
            "col",
            lax.rem(col + o, cols),
        )
        for o in range(1, cols)
    ]
    total = terms[col] + noise[0] * direction[...]
    for o, copy in enumerate(copies, 1):
        copy.wait()
        total = total + parts[lax.rem(col + cols - o, cols)]
    curvature = jnp.sum(direction[...] * total, axis=1, keepdims=True)
    curve[0] = jnp.broadcast_to(curvature, curve.shape[1:])
    curve[1] = total_over(curve.at[0], curve_cols, sems.at[0, 1], sems.at[1, 1], "col", cols)
    curvature = total_over(curve.at[1], curve_rows, sems.at[0, 2], sems.at[1, 2], "row", rows)
    step_size = (previous[...] / curvature)[:, :1]
    new_iterate[...] = iterate[...] + step_size * direction[...]
    updated = residual[...] - step_size * total
    new_residual[...] = updated
    everyone[col, row] = updated.astype(jnp.bfloat16)

    partner = col + 1 - 2 * lax.rem(col, 2)
    waits, row_copies, chip_copies = [], [], []
    for o in range(1, rows):
        slot = everyone.at[col, row]
        row_copies.append(
            push(slot, slot, row_sems.at[0, o], row_sems.at[1, o], "row", lax.rem(row + o, rows))
        )
    chips = cols // 2
    for o in range(rows):
        if o:
            row_copies[o - 1].wait_recv()
        slot = everyone.at[col, lax.rem(row + rows - o, rows)]
        for e in range(1, chips):
            chip_copies.append(
                (
                    o,
                    e,
                    push(
                        slot,
                        slot,
                        chip_sems.at[0, e, o],
                        chip_sems.at[1, e, o],
                        "col",
                        lax.rem(col + 2 * e, cols),
                    ),
                )
            )
        waits.append(
            push(slot, slot, core_sems.at[0, 0, o], core_sems.at[1, 0, o], "col", partner)
        )
    for o, e, copy in chip_copies:
        copy.wait_recv()
        slot = everyone.at[lax.rem(col + cols - 2 * e, cols), lax.rem(row + rows - o, rows)]
        waits.append(
            push(slot, slot, core_sems.at[0, e, o], core_sems.at[1, e, o], "col", partner)
        )
    for copy in row_copies:
        copy.wait_send()
    for _, _, copy in chip_copies:
        copy.wait_send()
    for copy in waits:
        copy.wait()


def take_step(terms, direction, residual, iterate, previous, noise, rows, cols):
    probes, own_count = direction.shape
    widest = max(rows, cols)
    vmem = pl.BlockSpec(memory_space=pltpu.VMEM)

    def kernel(*refs):
        step_kernel(rows, cols, *refs)

    return pl.pallas_call(
        kernel,
        out_shape=[
            jax.ShapeDtypeStruct((probes, own_count), jnp.float32),
            jax.ShapeDtypeStruct((probes, own_count), jnp.float32),
            jax.ShapeDtypeStruct((cols, rows, probes, own_count), jnp.bfloat16),
        ],
        in_specs=[vmem] * 5 + [pl.BlockSpec(memory_space=pltpu.SMEM)],
        out_specs=[vmem] * 3,
        scratch_shapes=[
            pltpu.VMEM((cols, probes, own_count), jnp.float32),
            pltpu.VMEM((2, probes, 128), jnp.float32),
            pltpu.VMEM((cols, probes, 128), jnp.float32),
            pltpu.VMEM((rows, probes, 128), jnp.float32),
            pltpu.SemaphoreType.DMA((2, 3, widest)),
            pltpu.SemaphoreType.DMA((2, rows)),
            pltpu.SemaphoreType.DMA((2, cols // 2, rows)),
            pltpu.SemaphoreType.DMA((2, cols // 2, rows)),
        ],
        compiler_params=pltpu.CompilerParams(collective_id=2, has_side_effects=True),
    )(terms, direction, residual, iterate, previous, noise)


def cluster_kernel(
    rows,
    cols,
    everyone,
    local,
    present,
    origin,
    wanted,
    direction,
    previous,
    factors,
    new_direction,
    rz_out,
    held,
    inner_parts,
    inner_got,
    inner_all,
    outer_cols,
    outgoing,
    incoming,
    rz,
    rz_cols,
    rz_rows,
    load_sems,
    part_sems,
    sems,
):
    row, col = lax.axis_index("row"), lax.axis_index("col")
    slots, length, width = held.shape
    probes, own_count = direction.shape
    parts = CORE // own_count
    pieces = own_count // width
    loads = [
        pltpu.make_async_copy(factors.at[s], held.at[s], load_sems.at[s]) for s in range(slots)
    ]
    for load in loads:
        load.start()
    greet({"row": rows, "col": cols})

    chosen, copies = [], []
    position = lax.broadcasted_iota(jnp.int32, (CORE, width), 0)
    for s in range(slots):
        block = [everyone[origin[0, s] + p, origin[1, s]] for p in range(parts)]
        block = jnp.concatenate(block, axis=1) if parts > 1 else block[0]
        pick = jnp.where(position == local[s : s + 1, :], 1.0, 0.0).astype(jnp.bfloat16)
        values = jnp.dot(block, pick, preferred_element_type=jnp.float32).astype(jnp.bfloat16)
        chosen.append(values)
        loads[s].wait()
        inner = lax.dot_general(
            values, held[s], (((1,), (1,)), ((), ())), preferred_element_type=jnp.float32
        )
        for k in range(cols):
            inner_parts[k, s] = inner[:, k * width : (k + 1) * width]
        for o in range(1, cols):
            peer = lax.rem(col + o, cols)
            copies.append(
                push(
                    inner_parts.at[peer, s],
                    inner_got.at[col, s],
                    part_sems.at[0, s, o],
                    part_sems.at[1, s, o],
                    "col",
                    peer,
                )
            )
    for copy in copies:
        copy.wait()
    for s in range(slots):
        inner = inner_parts[col, s]
        for o in range(1, cols):
            inner = inner + inner_got[lax.rem(col + o, cols), s]
        inner_all[col, s] = (inner * present[s : s + 1, :]).astype(jnp.bfloat16)
    mine = inner_all.at[col]
    for copy in spread(mine, inner_all, sems.at[0, 0], sems.at[1, 0], "col", cols):
        copy.wait()
    rz_part = jnp.zeros((probes, 1), jnp.float32)
    for s in range(slots):
        inner = jnp.concatenate([inner_all[k, s] for k in range(cols)], axis=1)
        outer = jnp.dot(inner, held[s], preferred_element_type=jnp.float32)
        outer_cols[col, s] = outer.astype(jnp.bfloat16)
        rz_part += jnp.sum(chosen[s].astype(jnp.float32) * outer, axis=1, keepdims=True)
    is_core = jnp.where(col * width < CORE, 1.0, 0.0)
    rz[0] = jnp.broadcast_to(rz_part * is_core, rz.shape[1:])
    mine = outer_cols.at[col]
    copies = spread(mine, outer_cols, sems.at[0, 1], sems.at[1, 1], "col", cols)
    rz[1] = total_over(rz.at[0], rz_cols, sems.at[0, 2], sems.at[1, 2], "col", cols)
    for copy in copies:
        copy.wait()
    first = lax.rem(col, parts) * pieces
    for n in range(pieces):
        values = [outer_cols[first + n, s].astype(jnp.float32) for s in range(slots)]
        for r in range(rows):
            total = jnp.zeros((probes, width), jnp.float32)
            for s in range(slots):
                total = total + wanted[r, s] * values[s]
            outgoing[r, n] = total.astype(jnp.bfloat16)
    copies = [
        push(
            outgoing.at[lax.rem(row + o, rows)],
            incoming.at[row],
            sems.at[0, 3, o],
            sems.at[1, 3, o],
            "row",
            lax.rem(row + o, rows),
        )
        for o in range(1, rows)
    ]
    incoming[row] = outgoing[row]
    total = total_over(rz.at[1], rz_rows, sems.at[0, 4], sems.at[1, 4], "row", rows)
    rz_out[...] = total
    ratio = (total / previous[...])[:, :1]
    for copy in copies:
        copy.wait()
    for n in range(pieces):
        precond = incoming[0, n].astype(jnp.float32)
        for r in range(1, rows):
            precond = precond + incoming[r, n].astype(jnp.float32)
        span = slice(n * width, (n + 1) * width)
        new_direction[:, span] = precond + ratio * direction[:, span]


def apply_clusters(everyone, local, present, origin, wanted, direction, previous, factors):
    cols, rows, probes, own_count = everyone.shape
    slots, length, width = factors.shape
    pieces = own_count // width
    widest = max(rows, cols)
    vmem = pl.BlockSpec(memory_space=pltpu.VMEM)
    smem = pl.BlockSpec(memory_space=pltpu.SMEM)

    def kernel(*refs):
        cluster_kernel(rows, cols, *refs)

    return pl.pallas_call(
        kernel,
        out_shape=[
            jax.ShapeDtypeStruct((probes, own_count), jnp.float32),
            jax.ShapeDtypeStruct((probes, 128), jnp.float32),
        ],
        in_specs=[vmem, vmem, vmem, smem, smem, vmem, vmem, pl.BlockSpec(memory_space=pl.ANY)],
        out_specs=[vmem] * 2,
        scratch_shapes=[
            pltpu.VMEM((slots, length, width), jnp.bfloat16),
            pltpu.VMEM((cols, slots, probes, width), jnp.float32),
            pltpu.VMEM((cols, slots, probes, width), jnp.float32),
            pltpu.VMEM((cols, slots, probes, width), jnp.bfloat16),
            pltpu.VMEM((cols, slots, probes, width), jnp.bfloat16),
            pltpu.VMEM((rows, pieces, probes, width), jnp.bfloat16),
            pltpu.VMEM((rows, pieces, probes, width), jnp.bfloat16),
            pltpu.VMEM((2, probes, 128), jnp.float32),
            pltpu.VMEM((cols, probes, 128), jnp.float32),
            pltpu.VMEM((rows, probes, 128), jnp.float32),
            pltpu.SemaphoreType.DMA((slots,)),
            pltpu.SemaphoreType.DMA((2, slots, cols)),
            pltpu.SemaphoreType.DMA((2, 5, widest)),
        ],
        compiler_params=pltpu.CompilerParams(collective_id=3, has_side_effects=True),
    )(everyone, local, present, origin, wanted, direction, previous, factors)


def lanes(values):
    return jnp.broadcast_to(values[:, None], (values.shape[0], 128))


def on_device(
    points,
    lengthscale,
    noise,
    iterate,
    residual,
    direction,
    previous_rz,
    members,
    slot_cluster,
    factors,
):
    own_count = direction.shape[1]
    rows, cols = lax.axis_size("row"), lax.axis_size("col")
    point_count = rows * cols * own_count
    col = lax.axis_index("col")
    own_width = factors.shape[2]
    parts = CORE // own_count

    scaled = points / lengthscale[:, None] * SPREAD
    direction_low = direction.astype(jnp.bfloat16)
    column_points, column_vectors, row_points = exchange(
        [(scaled, "row", "gather"), (direction_low, "row", "gather"), (scaled, "col", "gather")], 1
    )
    terms = apply_tile(row_points, column_points, column_vectors)
    previous = lanes(previous_rz)
    new_iterate, new_residual, everyone = take_step(
        terms, direction, residual, iterate, previous, noise, rows, cols
    )

    slot_cluster, members, _ = lax.optimization_barrier((slot_cluster, members, column_points))
    own_members = lax.dynamic_slice_in_dim(members, col * own_width, own_width, 1)
    own_ids = jnp.take(own_members, slot_cluster, axis=0)
    source = jnp.minimum(jnp.min(own_ids, axis=1), point_count - 1) // CORE
    local = own_ids - source[:, None] * CORE
    present = (own_ids < point_count).astype(jnp.float32)
    first = source * parts
    origin = jnp.stack([first % cols, first // cols])
    devices = jnp.arange(rows, dtype=jnp.int32) * cols + col
    wanted = ((devices // parts)[:, None] == slot_cluster[None, :]).astype(jnp.float32)
    new_direction, rz_lanes = apply_clusters(
        everyone, local, present, origin, wanted, direction, previous, factors
    )
    return (new_iterate, new_residual, new_direction, rz_lanes[:, 0])


def solution(mesh):
    placed = (
        P(None, ("row", "col")),
        P(),
        P(),
        P(None, ("row", "col")),
        P(None, ("row", "col")),
        P(None, ("row", "col")),
        P(),
        P(),
        P("row"),
        P("row", None, "col"),
    )
    return jax.shard_map(
        on_device,
        mesh=mesh,
        in_specs=placed,
        out_specs=(P(None, ("row", "col")), P(None, ("row", "col")), P(None, ("row", "col")), P()),
        check_vma=False,
    )
```

```python
import math

import jax
import jax.numpy as jnp
from jax import lax
from jax.experimental import pallas as pl
from jax.experimental.pallas import tpu as pltpu
from jax.sharding import PartitionSpec as P

CORE = 1024
MESH = pl.DeviceIdType.MESH
FEATURES = 64
LOG2E = math.log2(math.e)
SPREAD = math.sqrt(5.0) * LOG2E
SHIFT = 1.5 * LOG2E
LIFT = 0.75 * LOG2E * LOG2E
EXPONENT = -math.log2(3.0 * LOG2E * LOG2E)


def exchange(arrays, collective_id):
    sizes = {axis: lax.axis_size(axis) for _, axis, _ in arrays}
    count = len(arrays)
    widest = max(sizes.values())

    def kernel(*refs):
        sources, targets = refs[:count], refs[count : 2 * count]
        send_sem, recv_sem = refs[2 * count :]
        barrier = pltpu.get_barrier_semaphore()
        for axis, size in sizes.items():
            me = lax.axis_index(axis)
            for offset in range(1, size):
                pl.semaphore_signal(
                    barrier,
                    inc=1,
                    device_id={axis: lax.rem(me + offset, size)},
                    device_id_type=MESH,
                )
        pl.semaphore_wait(barrier, sum(size - 1 for size in sizes.values()))
        copies = []
        for offset in range(1, widest):
            for k, (_, axis, mode) in enumerate(arrays):
                size = sizes[axis]
                if offset >= size:
                    continue
                me = lax.axis_index(axis)
                peer = lax.rem(me + offset, size)
                copy = pltpu.make_async_remote_copy(
                    src_ref=sources[k] if mode == "gather" else sources[k].at[peer],
                    dst_ref=targets[k].at[me],
                    send_sem=send_sem.at[k, offset],
                    recv_sem=recv_sem.at[k, offset],
                    device_id={axis: peer},
                    device_id_type=MESH,
                )
                copy.start()
                copies.append(copy)
        for k, (_, axis, mode) in enumerate(arrays):
            me = lax.axis_index(axis)
            targets[k][me] = sources[k][...] if mode == "gather" else sources[k][me]
        for copy in copies:
            copy.wait()

    shapes = []
    for array, axis, mode in arrays:
        shape = (sizes[axis],) + array.shape if mode == "gather" else array.shape
        shapes.append(jax.ShapeDtypeStruct(shape, array.dtype))
    return pl.pallas_call(
        kernel,
        out_shape=shapes,
        in_specs=[pl.BlockSpec(memory_space=pltpu.VMEM)] * count,
        out_specs=[pl.BlockSpec(memory_space=pltpu.VMEM)] * count,
        scratch_shapes=[
            pltpu.SemaphoreType.DMA((count, widest)),
            pltpu.SemaphoreType.DMA((count, widest)),
        ],
        compiler_params=pltpu.CompilerParams(collective_id=collective_id, has_side_effects=True),
    )(*[array for array, _, _ in arrays])


def split_three(values):
    high = values.astype(jnp.bfloat16).astype(jnp.float32)
    rest = values - high
    middle = rest.astype(jnp.bfloat16).astype(jnp.float32)
    return high, middle, rest - middle


def feature_rows(points, left):
    high, middle, low = split_three(points)
    norms = split_three(jnp.sum(points * points, axis=0, keepdims=True))
    row = lax.broadcasted_iota(jnp.int32, points.shape, 0)
    first = 0 if left else 3
    tail = jnp.where(row < 6, 1.0, 0.0)
    for k in range(3):
        tail = jnp.where(row == first + k, norms[k], tail)
    if left:
        parts = [-2.0 * part for part in (high, high, middle, middle, high, low)]
    else:
        parts = [high, middle, high, middle, low, high]
    parts += [tail, jnp.zeros_like(tail)]
    return jnp.concatenate(parts, axis=0)


def tile_kernel(
    tile, left_points, right_points, left_vectors, right_vectors, out_left, out_right, *scratch
):
    left, right, flipped, sums = scratch
    row, col = lax.axis_index("row"), lax.axis_index("col")
    cols, _, own_count = left_points.shape
    rows = right_points.shape[0]
    half = rows // 2
    per_block = own_count // tile

    def build_left(c, carry):
        left[c] = feature_rows(left_points[c], True).astype(jnp.bfloat16)
        flipped[c] = jnp.transpose(left_vectors[c].astype(jnp.float32)).astype(jnp.bfloat16)
        return carry

    def build_right(ahead, carry):
        features = feature_rows(right_points[lax.rem(row + ahead, rows)], False)
        right[ahead] = jnp.transpose(features).astype(jnp.bfloat16)
        return carry

    lax.fori_loop(0, cols, build_left, 0)
    lax.fori_loop(0, half + 1, build_right, 0)
    out_left[...] = jnp.zeros_like(out_left)
    sums[...] = jnp.zeros_like(sums)

    def apply(c, ahead, part, both):
        start = pl.multiple_of(part * tile, tile)
        squared = jnp.dot(
            right[ahead, pl.ds(start, tile), :], left[c], preferred_element_type=jnp.float32
        )
        squared = jnp.maximum(squared, 1e-30)
        radius = squared * lax.rsqrt(squared)
        shifted = radius + SHIFT
        kernel = ((shifted * shifted + LIFT) * jnp.exp2(EXPONENT - radius)).astype(jnp.bfloat16)
        out_left[c] += jnp.dot(
            right_vectors[lax.rem(row + ahead, rows), :, pl.ds(start, tile)],
            kernel,
            preferred_element_type=jnp.float32,
        )
        other = jnp.dot(kernel, flipped[c], preferred_element_type=jnp.float32)
        sums[ahead, pl.ds(start, tile), :] += both * other

    def step(index, carry):
        pair, part = index // per_block, lax.rem(index, per_block)
        c, ahead = lax.rem(pair, cols), pair // cols
        ahead = jnp.where(ahead > 0, ahead, jnp.where(c <= col, 0, half))
        same = jnp.logical_and(ahead == 0, c == col)
        apply(c, ahead, part, jnp.where(same, 0.0, 1.0))
        return carry

    lax.fori_loop(0, half * cols * per_block, step, 0)

    @pl.when(row < half)
    def _():
        def last(part, carry):
            apply(col, half, part, 1.0)
            return carry

        lax.fori_loop(0, per_block, last, 0)

    for ahead in range(half + 1):
        out_right[ahead] = jnp.transpose(sums[ahead])


def apply_tile(left_points, right_points, left_vectors, right_vectors):
    cols, probes, own_count = left_vectors.shape
    rows = right_vectors.shape[0]
    half = rows // 2
    tile = math.gcd(1024, own_count)
    vmem = pl.BlockSpec(memory_space=pltpu.VMEM)

    def kernel(*refs):
        tile_kernel(tile, *refs)

    return pl.pallas_call(
        kernel,
        out_shape=[
            jax.ShapeDtypeStruct((cols, probes, own_count), jnp.float32),
            jax.ShapeDtypeStruct((half + 1, probes, own_count), jnp.float32),
        ],
        in_specs=[vmem] * 4,
        out_specs=[vmem] * 2,
        scratch_shapes=[
            pltpu.VMEM((cols, FEATURES, own_count), jnp.bfloat16),
            pltpu.VMEM((half + 1, own_count, FEATURES), jnp.bfloat16),
            pltpu.VMEM((cols, own_count, probes), jnp.bfloat16),
            pltpu.VMEM((half + 1, own_count, probes), jnp.float32),
        ],
    )(left_points, right_points, left_vectors, right_vectors)


def greet(sizes):
    barrier = pltpu.get_barrier_semaphore()
    for axis, size in sizes.items():
        me = lax.axis_index(axis)
        for offset in range(1, size):
            pl.semaphore_signal(
                barrier,
                inc=1,
                device_id={axis: lax.rem(me + offset, size)},
                device_id_type=MESH,
            )
    pl.semaphore_wait(barrier, sum(size - 1 for size in sizes.values()))


def push(source, target, send_sem, recv_sem, axis, peer):
    copy = pltpu.make_async_remote_copy(
        src_ref=source,
        dst_ref=target,
        send_sem=send_sem,
        recv_sem=recv_sem,
        device_id={axis: peer},
        device_id_type=MESH,
    )
    copy.start()
    return copy


def spread(source, target, send_sem, recv_sem, axis, size):
    me = lax.axis_index(axis)
    return [
        push(source, target.at[me], send_sem.at[o], recv_sem.at[o], axis, lax.rem(me + o, size))
        for o in range(1, size)
    ]


def total_over(mine, held, send_sem, recv_sem, axis, size):
    copies = spread(mine, held, send_sem, recv_sem, axis, size)
    held[lax.axis_index(axis)] = mine[...]
    for copy in copies:
        copy.wait()
    total = held[0]
    for k in range(1, size):
        total = total + held[k]
    return total


def step_kernel(
    rows,
    cols,
    terms,
    others,
    direction,
    residual,
    iterate,
    previous,
    noise,
    new_iterate,
    new_residual,
    everyone,
    parts,
    other_parts,
    curve,
    curve_cols,
    curve_rows,
    sems,
    row_sems,
    chip_sems,
    core_sems,
):
    row, col = lax.axis_index("row"), lax.axis_index("col")
    greet({"row": rows, "col": cols})
    copies = [
        push(
            terms.at[lax.rem(col + o, cols)],
            parts.at[col],
            sems.at[0, 0, o],
            sems.at[1, 0, o],
            "col",
            lax.rem(col + o, cols),
        )
        for o in range(1, cols)
    ]
    other_copies = [
        push(
            others.at[ahead],
            other_parts.at[ahead],
            sems.at[0, 3, ahead],
            sems.at[1, 3, ahead],
            "row",
            lax.rem(row + ahead, rows),
        )
        for ahead in range(1, rows // 2 + 1)
    ]
    total = terms[col] + others[0] + noise[0] * direction[...]
    for o, copy in enumerate(copies, 1):
        copy.wait()
        total = total + parts[lax.rem(col + cols - o, cols)]
    for ahead, copy in enumerate(other_copies, 1):
        copy.wait()
        total = total + other_parts[ahead]
    curvature = jnp.sum(direction[...] * total, axis=1, keepdims=True)
    curve[0] = jnp.broadcast_to(curvature, curve.shape[1:])
    curve[1] = total_over(curve.at[0], curve_cols, sems.at[0, 1], sems.at[1, 1], "col", cols)
    curvature = total_over(curve.at[1], curve_rows, sems.at[0, 2], sems.at[1, 2], "row", rows)
    step_size = (previous[...] / curvature)[:, :1]
    new_iterate[...] = iterate[...] + step_size * direction[...]
    updated = residual[...] - step_size * total
    new_residual[...] = updated
    everyone[col, row] = updated.astype(jnp.bfloat16)

    partner = col + 1 - 2 * lax.rem(col, 2)
    waits, row_copies, chip_copies = [], [], []
    for o in range(1, rows):
        slot = everyone.at[col, row]
        row_copies.append(
            push(slot, slot, row_sems.at[0, o], row_sems.at[1, o], "row", lax.rem(row + o, rows))
        )
    chips = cols // 2
    for o in range(rows):
        if o:
            row_copies[o - 1].wait_recv()
        slot = everyone.at[col, lax.rem(row + rows - o, rows)]
        for e in range(1, chips):
            chip_copies.append(
                (
                    o,
                    e,
                    push(
                        slot,
                        slot,
                        chip_sems.at[0, e, o],
                        chip_sems.at[1, e, o],
                        "col",
                        lax.rem(col + 2 * e, cols),
                    ),
                )
            )
        waits.append(
            push(slot, slot, core_sems.at[0, 0, o], core_sems.at[1, 0, o], "col", partner)
        )
    for o, e, copy in chip_copies:
        copy.wait_recv()
        slot = everyone.at[lax.rem(col + cols - 2 * e, cols), lax.rem(row + rows - o, rows)]
        waits.append(
            push(slot, slot, core_sems.at[0, e, o], core_sems.at[1, e, o], "col", partner)
        )
    for copy in row_copies:
        copy.wait_send()
    for _, _, copy in chip_copies:
        copy.wait_send()
    for copy in waits:
        copy.wait()


def take_step(terms, others, direction, residual, iterate, previous, noise, rows, cols):
    probes, own_count = direction.shape
    widest = max(rows, cols)
    vmem = pl.BlockSpec(memory_space=pltpu.VMEM)

    def kernel(*refs):
        step_kernel(rows, cols, *refs)

    return pl.pallas_call(
        kernel,
        out_shape=[
            jax.ShapeDtypeStruct((probes, own_count), jnp.float32),
            jax.ShapeDtypeStruct((probes, own_count), jnp.float32),
            jax.ShapeDtypeStruct((cols, rows, probes, own_count), jnp.bfloat16),
        ],
        in_specs=[vmem] * 6 + [pl.BlockSpec(memory_space=pltpu.SMEM)],
        out_specs=[vmem] * 3,
        scratch_shapes=[
            pltpu.VMEM((cols, probes, own_count), jnp.float32),
            pltpu.VMEM(others.shape, jnp.float32),
            pltpu.VMEM((2, probes, 128), jnp.float32),
            pltpu.VMEM((cols, probes, 128), jnp.float32),
            pltpu.VMEM((rows, probes, 128), jnp.float32),
            pltpu.SemaphoreType.DMA((2, 4, widest)),
            pltpu.SemaphoreType.DMA((2, rows)),
            pltpu.SemaphoreType.DMA((2, cols // 2, rows)),
            pltpu.SemaphoreType.DMA((2, cols // 2, rows)),
        ],
        compiler_params=pltpu.CompilerParams(collective_id=2, has_side_effects=True),
    )(terms, others, direction, residual, iterate, previous, noise)


def cluster_kernel(
    rows,
    cols,
    everyone,
    local,
    present,
    origin,
    wanted,
    direction,
    previous,
    factors,
    new_direction,
    rz_out,
    held,
    inner_parts,
    inner_got,
    inner_all,
    outer_cols,
    outgoing,
    incoming,
    rz,
    rz_cols,
    rz_rows,
    load_sems,
    part_sems,
    sems,
):
    row, col = lax.axis_index("row"), lax.axis_index("col")
    slots, length, width = held.shape
    probes, own_count = direction.shape
    parts = CORE // own_count
    pieces = own_count // width
    loads = [
        pltpu.make_async_copy(factors.at[s], held.at[s], load_sems.at[s]) for s in range(slots)
    ]
    for load in loads:
        load.start()
    greet({"row": rows, "col": cols})

    chosen, copies = [], []
    position = lax.broadcasted_iota(jnp.int32, (CORE, width), 0)
    for s in range(slots):
        block = [everyone[origin[0, s] + p, origin[1, s]] for p in range(parts)]
        block = jnp.concatenate(block, axis=1) if parts > 1 else block[0]
        pick = jnp.where(position == local[s : s + 1, :], 1.0, 0.0).astype(jnp.bfloat16)
        values = jnp.dot(block, pick, preferred_element_type=jnp.float32).astype(jnp.bfloat16)
        chosen.append(values)
        loads[s].wait()
        inner = lax.dot_general(
            values, held[s], (((1,), (1,)), ((), ())), preferred_element_type=jnp.float32
        )
        for k in range(cols):
            inner_parts[k, s] = inner[:, k * width : (k + 1) * width]
        for o in range(1, cols):
            peer = lax.rem(col + o, cols)
            copies.append(
                push(
                    inner_parts.at[peer, s],
                    inner_got.at[col, s],
                    part_sems.at[0, s, o],
                    part_sems.at[1, s, o],
                    "col",
                    peer,
                )
            )
    for copy in copies:
        copy.wait()
    for s in range(slots):
        inner = inner_parts[col, s]
        for o in range(1, cols):
            inner = inner + inner_got[lax.rem(col + o, cols), s]
        inner_all[col, s] = (inner * present[s : s + 1, :]).astype(jnp.bfloat16)
    mine = inner_all.at[col]
    for copy in spread(mine, inner_all, sems.at[0, 0], sems.at[1, 0], "col", cols):
        copy.wait()
    rz_part = jnp.zeros((probes, 1), jnp.float32)
    for s in range(slots):
        inner = jnp.concatenate([inner_all[k, s] for k in range(cols)], axis=1)
        outer = jnp.dot(inner, held[s], preferred_element_type=jnp.float32)
        outer_cols[col, s] = outer.astype(jnp.bfloat16)
        rz_part += jnp.sum(chosen[s].astype(jnp.float32) * outer, axis=1, keepdims=True)
    is_core = jnp.where(col * width < CORE, 1.0, 0.0)
    rz[0] = jnp.broadcast_to(rz_part * is_core, rz.shape[1:])
    mine = outer_cols.at[col]
    copies = spread(mine, outer_cols, sems.at[0, 1], sems.at[1, 1], "col", cols)
    rz[1] = total_over(rz.at[0], rz_cols, sems.at[0, 2], sems.at[1, 2], "col", cols)
    for copy in copies:
        copy.wait()
    first = lax.rem(col, parts) * pieces
    for n in range(pieces):
        values = [outer_cols[first + n, s].astype(jnp.float32) for s in range(slots)]
        for r in range(rows):
            total = jnp.zeros((probes, width), jnp.float32)
            for s in range(slots):
                total = total + wanted[r, s] * values[s]
            outgoing[r, n] = total.astype(jnp.bfloat16)
    copies = [
        push(
            outgoing.at[lax.rem(row + o, rows)],
            incoming.at[row],
            sems.at[0, 3, o],
            sems.at[1, 3, o],
            "row",
            lax.rem(row + o, rows),
        )
        for o in range(1, rows)
    ]
    incoming[row] = outgoing[row]
    total = total_over(rz.at[1], rz_rows, sems.at[0, 4], sems.at[1, 4], "row", rows)
    rz_out[...] = total
    ratio = (total / previous[...])[:, :1]
    for copy in copies:
        copy.wait()
    for n in range(pieces):
        precond = incoming[0, n].astype(jnp.float32)
        for r in range(1, rows):
            precond = precond + incoming[r, n].astype(jnp.float32)
        span = slice(n * width, (n + 1) * width)
        new_direction[:, span] = precond + ratio * direction[:, span]


def apply_clusters(everyone, local, present, origin, wanted, direction, previous, factors):
    cols, rows, probes, own_count = everyone.shape
    slots, length, width = factors.shape
    pieces = own_count // width
    widest = max(rows, cols)
    vmem = pl.BlockSpec(memory_space=pltpu.VMEM)
    smem = pl.BlockSpec(memory_space=pltpu.SMEM)

    def kernel(*refs):
        cluster_kernel(rows, cols, *refs)

    return pl.pallas_call(
        kernel,
        out_shape=[
            jax.ShapeDtypeStruct((probes, own_count), jnp.float32),
            jax.ShapeDtypeStruct((probes, 128), jnp.float32),
        ],
        in_specs=[vmem, vmem, vmem, smem, smem, vmem, vmem, pl.BlockSpec(memory_space=pl.ANY)],
        out_specs=[vmem] * 2,
        scratch_shapes=[
            pltpu.VMEM((slots, length, width), jnp.bfloat16),
            pltpu.VMEM((cols, slots, probes, width), jnp.float32),
            pltpu.VMEM((cols, slots, probes, width), jnp.float32),
            pltpu.VMEM((cols, slots, probes, width), jnp.bfloat16),
            pltpu.VMEM((cols, slots, probes, width), jnp.bfloat16),
            pltpu.VMEM((rows, pieces, probes, width), jnp.bfloat16),
            pltpu.VMEM((rows, pieces, probes, width), jnp.bfloat16),
            pltpu.VMEM((2, probes, 128), jnp.float32),
            pltpu.VMEM((cols, probes, 128), jnp.float32),
            pltpu.VMEM((rows, probes, 128), jnp.float32),
            pltpu.SemaphoreType.DMA((slots,)),
            pltpu.SemaphoreType.DMA((2, slots, cols)),
            pltpu.SemaphoreType.DMA((2, 5, widest)),
        ],
        compiler_params=pltpu.CompilerParams(collective_id=3, has_side_effects=True),
    )(everyone, local, present, origin, wanted, direction, previous, factors)


def lanes(values):
    return jnp.broadcast_to(values[:, None], (values.shape[0], 128))


def on_device(
    points,
    lengthscale,
    noise,
    iterate,
    residual,
    direction,
    previous_rz,
    members,
    slot_cluster,
    factors,
):
    own_count = direction.shape[1]
    rows, cols = lax.axis_size("row"), lax.axis_size("col")
    point_count = rows * cols * own_count
    col = lax.axis_index("col")
    own_width = factors.shape[2]
    parts = CORE // own_count

    scaled = points / lengthscale[:, None] * SPREAD
    direction_low = direction.astype(jnp.bfloat16)
    column_points, column_vectors, row_points, row_vectors = exchange(
        [
            (scaled, "row", "gather"),
            (direction_low, "row", "gather"),
            (scaled, "col", "gather"),
            (direction_low, "col", "gather"),
        ],
        1,
    )
    terms, others = apply_tile(row_points, column_points, row_vectors, column_vectors)
    previous = lanes(previous_rz)
    new_iterate, new_residual, everyone = take_step(
        terms, others, direction, residual, iterate, previous, noise, rows, cols
    )

    slot_cluster, members, _ = lax.optimization_barrier((slot_cluster, members, column_points))
    own_members = lax.dynamic_slice_in_dim(members, col * own_width, own_width, 1)
    own_ids = jnp.take(own_members, slot_cluster, axis=0)
    source = jnp.minimum(jnp.min(own_ids, axis=1), point_count - 1) // CORE
    local = own_ids - source[:, None] * CORE
    present = (own_ids < point_count).astype(jnp.float32)
    first = source * parts
    origin = jnp.stack([first % cols, first // cols])
    devices = jnp.arange(rows, dtype=jnp.int32) * cols + col
    wanted = ((devices // parts)[:, None] == slot_cluster[None, :]).astype(jnp.float32)
    new_direction, rz_lanes = apply_clusters(
        everyone, local, present, origin, wanted, direction, previous, factors
    )
    return (new_iterate, new_residual, new_direction, rz_lanes[:, 0])


def solution(mesh):
    placed = (
        P(None, ("row", "col")),
        P(),
        P(),
        P(None, ("row", "col")),
        P(None, ("row", "col")),
        P(None, ("row", "col")),
        P(),
        P(),
        P("row"),
        P("row", None, "col"),
    )
    return jax.shard_map(
        on_device,
        mesh=mesh,
        in_specs=placed,
        out_specs=(P(None, ("row", "col")), P(None, ("row", "col")), P(None, ("row", "col")), P()),
        check_vma=False,
    )
```
